32 devices in a mesh: groups: 2 (over x), mp: 16 (over z, y, core).
Axes of the slice: x: 2, y: 2, z: 4, core: 2. Of those that a mesh axis runs over, the one named last changes fastest.
Arguments:
- tokens: bfloat16 [512, 8192], P(('groups', 'mp')), parts along dimension 0, may hold values from -6 to 6
- queries: bfloat16 [512, 8192], P(('groups', 'mp')), parts along dimension 0, may hold values from -35 to 35
- key_proj: bfloat16 [512, 1024], P(('groups', 'mp')), parts along dimension 0, may hold values from -5 to 5
- values: bfloat16 [512, 1024], P(('groups', 'mp')), parts along dimension 0, may hold values from -6 to 6
- seq_lens: int32 [12], P('groups'), parts along dimension 0, may hold values from 21 to 85, as said below
- out_weight: bfloat16 [8192, 8192], P('mp'), may hold values from -0.25 to 0.25
- ffn_gain: float32 [2, 8192], replicated, may hold values from 0.25 to 2.5
- gate_weight: bfloat16 [8192, 12288], P(None, 'mp'), may hold values from -0.0625 to 0.0625
- up_weight: bfloat16 [8192, 12288], P(None, 'mp'), may hold values from -0.0625 to 0.0625
- down_weight: bfloat16 [12288, 8192], P('mp'), may hold values from -0.0546875 to 0.0546875
- slice_table: int32 [96], replicated, may hold values from 0 to 1, as said below
Outputs:
- stream: bfloat16 [512, 8192], P(('groups', 'mp')), parts along dimension 0
- mixed: bfloat16 [512, 8192], P(('groups', 'mp')), parts along dimension 0
The draws below stay inside these ranges and needn't reach their ends.
There are 2 independent parts, one for each index of `groups`. The reference program is written for one: setup_inputs(seed, part) draws one part's arguments, and reference() takes and returns one part's arrays. A program takes and returns all parts, laid end to end along the dimension named above; an argument that names none is the same for every part. Nothing has to cross between parts.
Inputs may be any that keep to these rules, and one draw needn't show every extreme that they name: `seq_lens`: the 6 lengths sum to 256; the shortest is exactly 21 and the longest exactly 85. `slice_table`: exactly 16 entries are 1, the rest 0.
All inputs are finite; a program needn't handle non-finite values.
Results may differ from the reference program's by a relative error of at most 0.02.
Values may be sent and summed in bfloat16 or wider, within the bound.
A program may use at most 128 MiB of HBM per device.

```python
import math
import jax
import jax.numpy as jnp
from jax import lax

D = 8192
QUERY_HEADS = 64
KEY_VALUE_HEADS = 8
HEAD_SIZE = 128
FA = 10240
JOINED = 2
SLICE = 128
SEQS = 6
WINDOW_TOKENS = 256
MIN_LEN = 21
MAX_LEN = 85
UNITS = 12288
SLICES = 96
N_MP = 16


def seq_lengths_from(key):
    base_key = jax.random.fold_in(key, 11)
    first_key, second_key, order_key = jax.random.split(base_key, 3)
    spare = WINDOW_TOKENS - MAX_LEN - 5 * MIN_LEN
    half_one = spare // 2
    half_two = spare - half_one
    cut_one = jax.random.randint(first_key, (), 0, half_one + 1).astype(jnp.int32)
    cut_two = jax.random.randint(second_key, (), 0, half_two + 1).astype(jnp.int32)
    middles = jnp.stack([cut_one, half_one - cut_one, cut_two, half_two - cut_two]).astype(jnp.int32) + MIN_LEN
    pieces = jnp.concatenate([jnp.full((1,), MIN_LEN, jnp.int32), jnp.full((1,), MAX_LEN, jnp.int32), middles])
    order = jax.random.permutation(order_key, SEQS)
    return pieces[order].astype(jnp.int32)


def query_key_pair(key):
    pair_key = jax.random.fold_in(key, 23)
    query_key, keys_random_seed = jax.random.split(pair_key, 2)
    query_out = jnp.clip(jax.random.normal(query_key, (WINDOW_TOKENS, QUERY_HEADS * HEAD_SIZE), jnp.float32), -5.0, 5.0)
    key_result = jnp.clip(jax.random.normal(keys_random_seed, (WINDOW_TOKENS, KEY_VALUE_HEADS * HEAD_SIZE), jnp.float32), -5.0, 5.0)
    return (query_out, key_result)


def draw_seq_lens(key, part):
    return seq_lengths_from(key)


def draw_queries(key, part):
    return query_key_pair(key)[0].astype(jnp.bfloat16)


def draw_key_proj(key, part):
    return query_key_pair(key)[1].astype(jnp.bfloat16)


def draw_slice_table(key, part):
    shuffled = jax.random.permutation(jax.random.fold_in(key, 31), SLICES)
    return (shuffled >= FA // SLICE).astype(jnp.int32)


def block_scale(own_key, dims, shards, least, high):
    def one(axis_at, parts):
        draws = jax.random.uniform(jax.random.fold_in(jax.random.fold_in(own_key, 6), axis_at), (parts,), jnp.float32, least / len(shards), high / len(shards))
        return jnp.repeat(jnp.exp(draws), dims[axis_at] // parts).reshape((-1,) + (1,) * (len(dims) - axis_at - 1))

    gain = one(*shards[0])
    for cut in shards[1:]:
        gain = gain * one(*cut)
    return gain


def gaussian(key, extent, deviation, reach, shards=(), kind=jnp.bfloat16):
    loudness = block_scale(key, extent, shards, -0.22, 0.18) if shards else 1.0
    entries = jax.random.normal(key, extent, jnp.float32) * deviation * loudness
    return jnp.minimum(jnp.maximum(entries, -reach), reach).astype(kind)


def setup_inputs(seed: int = 0, part: int = 0) -> dict:
    key_list = jax.random.split(jax.random.key(seed), 12)
    part_keys = jax.random.split(jax.random.fold_in(key_list[11], part), 12)
    return {
        "tokens": gaussian(part_keys[0], (WINDOW_TOKENS, D), 1.0, 6.0, ((0, 16),)),
        "queries": draw_queries(jax.random.fold_in(jax.random.fold_in(key_list[11], part), 71), part),
        "key_proj": draw_key_proj(jax.random.fold_in(jax.random.fold_in(key_list[11], part), 71), part),
        "values": gaussian(part_keys[3], (WINDOW_TOKENS, KEY_VALUE_HEADS * HEAD_SIZE), 1.0, 6.0, ((0, 16),)),
        "seq_lens": draw_seq_lens(jax.random.fold_in(jax.random.fold_in(key_list[11], part), 71), part),
        "out_weight": gaussian(key_list[5], (QUERY_HEADS * HEAD_SIZE, D), (QUERY_HEADS * HEAD_SIZE // 16) ** -0.5, 0.25, ((0, 16),)),
        "ffn_gain": jnp.clip(jnp.exp(jax.random.uniform(key_list[6], (JOINED, D), jnp.float32, math.log(0.25), math.log(2.5))), 0.25, 2.5),
        "gate_weight": gaussian(key_list[7], (D, UNITS), D ** -0.5, 0.0625, ((1, 16),)),
        "up_weight": gaussian(key_list[8], (D, UNITS), D ** -0.5, 0.0625, ((1, 16),)),
        "down_weight": gaussian(key_list[9], (UNITS, D), UNITS ** -0.5, 0.0546875, ((0, 16),)),
        "slice_table": draw_slice_table(jax.random.fold_in(key_list[11], 71), part),
    }


def reference(tokens, queries, key_proj, values, seq_lens, out_weight, ffn_gain, gate_weight, up_weight, down_weight, slice_table):
    positions = jnp.arange(WINDOW_TOKENS, dtype=jnp.int32)
    seq_ends = jnp.cumsum(seq_lens).astype(jnp.int32)
    segment_ids = lax.optimization_barrier(jnp.sum((positions[:, None] >= seq_ends[None, :]).astype(jnp.int32), axis=1))
    visible = (segment_ids[:, None] == segment_ids[None, :]) & (positions[None, :] <= positions[:, None])
    query_heads_per_group = QUERY_HEADS // KEY_VALUE_HEADS
    score_scale = 1.0 / math.sqrt(HEAD_SIZE)

    def one_head(head):
        query_cols = lax.dynamic_slice_in_dim(queries, (head * HEAD_SIZE).astype(jnp.int32), HEAD_SIZE, 1)
        kv_start = (head // query_heads_per_group * HEAD_SIZE).astype(jnp.int32)
        key_cols = lax.dynamic_slice_in_dim(key_proj, kv_start, HEAD_SIZE, 1)
        value_cols = lax.dynamic_slice_in_dim(values, kv_start, HEAD_SIZE, 1)
        scores = jnp.dot(query_cols, key_cols.T, preferred_element_type=jnp.float32) * score_scale
        masked = jnp.where(visible, scores, -1e+30)
        highest = lax.optimization_barrier(jnp.max(masked, axis=1, keepdims=True))
        expo = jnp.where(visible, jnp.exp(masked - highest), 0.0)
        attn_probs = (expo / lax.optimization_barrier(jnp.sum(expo, axis=1, keepdims=True))).astype(jnp.bfloat16)
        return jnp.dot(attn_probs, value_cols, preferred_element_type=jnp.float32).astype(jnp.bfloat16)
    context = lax.map(one_head, jnp.arange(QUERY_HEADS, dtype=jnp.int32))
    context = jnp.transpose(context, (1, 0, 2)).reshape(WINDOW_TOKENS, QUERY_HEADS * HEAD_SIZE)
    width_dev = QUERY_HEADS * HEAD_SIZE // N_MP

    def attn_group(running, group_idx):
        start_col = (group_idx * width_dev).astype(jnp.int32)
        cols = lax.dynamic_slice_in_dim(context, start_col, width_dev, 1)
        weight_rows = lax.dynamic_slice_in_dim(out_weight, start_col, width_dev, 0)
        term = jnp.dot(cols, weight_rows, preferred_element_type=jnp.float32).astype(jnp.bfloat16)
        term = lax.optimization_barrier(term)
        return (running + term.astype(jnp.float32), None)
    attn_sum, _ = lax.scan(attn_group, jnp.zeros((WINDOW_TOKENS, D), jnp.float32), jnp.arange(N_MP, dtype=jnp.int32))
    stream = (tokens.astype(jnp.float32) + attn_sum).astype(jnp.bfloat16)
    stream_full = stream.astype(jnp.float32)
    inv_rms = lax.rsqrt(lax.optimization_barrier(jnp.mean(stream_full * stream_full, axis=1, keepdims=True)) + 1e-05)
    normed = (stream_full * inv_rms).astype(jnp.bfloat16)
    gate_slices = jnp.transpose(gate_weight.reshape(D, SLICES, SLICE), (1, 0, 2))
    up_slices = jnp.transpose(up_weight.reshape(D, SLICES, SLICE), (1, 0, 2))

    def one_slice(packed):
        ffn_which, gate_cols, up_cols = packed
        gain_row = lax.dynamic_index_in_dim(ffn_gain, ffn_which, 0, keepdims=False)
        slice_input = (normed.astype(jnp.float32) * gain_row[None, :]).astype(jnp.bfloat16)
        gate_val = jnp.dot(slice_input, gate_cols, preferred_element_type=jnp.float32)
        up_val = jnp.dot(slice_input, up_cols, preferred_element_type=jnp.float32)
        return (jax.nn.silu(gate_val) * up_val).astype(jnp.bfloat16)
    hidden = lax.map(one_slice, (slice_table, gate_slices, up_slices))
    slices_dev = SLICES // N_MP
    hidden_groups = jnp.transpose(hidden.reshape(N_MP, slices_dev, WINDOW_TOKENS, SLICE), (0, 2, 1, 3)).reshape(N_MP, WINDOW_TOKENS, slices_dev * SLICE)
    down_groups = down_weight.reshape(N_MP, slices_dev * SLICE, D)

    def ffn_group(running, packed):
        hidden_rows, down_rows = packed
        term = jnp.dot(hidden_rows, down_rows, preferred_element_type=jnp.float32).astype(jnp.bfloat16)
        term = lax.optimization_barrier(term)
        return (running + term.astype(jnp.float32), None)
    ffn_sum, _ = lax.scan(ffn_group, jnp.zeros((WINDOW_TOKENS, D), jnp.float32), (hidden_groups, down_groups))
    mixed = (stream_full + ffn_sum).astype(jnp.bfloat16)
    return (stream, mixed)
```

```python
import functools
import math

import jax
import jax.numpy as jnp
import numpy as np
from jax import lax
from jax.experimental import pallas as pl
from jax.experimental.pallas import tpu as pltpu
from jax.sharding import PartitionSpec as P

QUERY_HEADS = 64
HEAD_SIZE = 128
SLICE = 128
CHUNKS = 8
MESH = pl.DeviceIdType.MESH
F32 = jnp.float32
BF16 = jnp.bfloat16


def place(zs):
    me = lax.axis_index("mp")
    core = lax.rem(me, 2)
    y = lax.rem(me // 2, 2)
    z = me // 4

    def dev(z_, y_, core_):
        return {"mp": (z_ * 2 + y_) * 2 + core_}

    return core, y, z, dev


def project_kernel(zs, gather, *refs):
    if gather:
        (a_ref, w_hbm, res_ref, out_ref, all_hbm, w, part, from_core, pair, from_y, quad, from_z,
         w_sem, cs, cr, ys, yr, zsend, zrecv, whole, gzs, gzr, gys, gyr, gcs, gcr, out_sem) = refs
    else:
        (a_ref, w_hbm, res_ref, out_ref, w, part, from_core, pair, from_y, quad, from_z,
         w_sem, cs, cr, ys, yr, zsend, zrecv) = refs
    core, y, z, dev = place(zs)
    n, half, cw = from_core.shape
    tok = half // 2 // zs

    def w_copy(j):
        cols = pl.ds(pl.multiple_of(j * cw, cw), cw)
        return pltpu.make_async_copy(w_hbm.at[:, cols], w.at[j], w_sem.at[j])

    def remote(src, dst, s, r, to):
        return pltpu.make_async_remote_copy(
            src_ref=src, dst_ref=dst, send_sem=s, recv_sem=r, device_id=to, device_id_type=MESH
        )

    def core_copy(j):
        return remote(part.at[j, 1 - core], from_core.at[j], cs.at[j], cr.at[j], dev(z, y, 1 - core))

    def y_copy(j):
        return remote(pair.at[j, 1 - y], from_y.at[j], ys.at[j], yr.at[j], dev(z, 1 - y, core))

    def z_copy(j, d):
        to = lax.rem(z + d, zs)
        return remote(
            quad.at[j, to], from_z.at[j, d], zsend.at[j, d], zrecv.at[j, d], dev(to, y, core)
        )

    def gz_copy(j, d):
        to = lax.rem(z + d, zs)
        mine = whole.at[j, core, y, z]
        return remote(mine, mine, gzs.at[j, d], gzr.at[j, d], dev(to, y, core))

    def gy_copy(j):
        mine = whole.at[j, core, y]
        return remote(mine, mine, gys.at[j], gyr.at[j], dev(z, 1 - y, core))

    def gc_copy(j):
        mine = whole.at[j, core]
        return remote(mine, mine, gcs.at[j], gcr.at[j], dev(z, y, 1 - core))

    def out_copy(j):
        return pltpu.make_async_copy(whole.at[j], all_hbm.at[j], out_sem.at[j])

    @pl.loop(0, n)
    def _(j):
        w_copy(j).start()

    barrier = pltpu.get_barrier_semaphore()
    partners = [dev(z, y, 1 - core), dev(z, 1 - y, core)]
    partners += [dev(lax.rem(z + d, zs), y, core) for d in range(1, zs)]
    for to in partners:
        pl.semaphore_signal(barrier, inc=1, device_id=to, device_id_type=MESH)
    pl.semaphore_wait(barrier, len(partners))

    def multiply(j):
        w_copy(j).wait()
        res = jnp.dot(a_ref[...], w[j], preferred_element_type=F32).astype(BF16)
        part[j, 0] = res[:half]
        part[j, 1] = res[half:]
        core_copy(j).start()

    def add_core(j):
        core_copy(j).wait_recv()
        res = (part[j, core].astype(F32) + from_core[j].astype(F32)).astype(BF16)
        pair[j, 0] = res[: half // 2]
        pair[j, 1] = res[half // 2 :]
        y_copy(j).start()

    def add_y(j):
        y_copy(j).wait_recv()
        res = (pair[j, y].astype(F32) + from_y[j].astype(F32)).astype(BF16)
        quad[j] = res.reshape(zs, tok, cw)
        for d in range(1, zs):
            z_copy(j, d).start()

    def add_z(j):
        total = quad[j, z].astype(F32)
        for d in range(1, zs):
            z_copy(j, d).wait_recv()
            total += from_z[j, d].astype(F32)
        cols = pl.ds(pl.multiple_of(j * cw, cw), cw)
        res = (res_ref[:, cols].astype(F32) + total).astype(BF16)
        out_ref[:, cols] = res
        if gather:
            whole[j, core, y, z] = res
            for d in range(1, zs):
                gz_copy(j, d).start()

    def spread_y(j):
        for d in range(1, zs):
            gz_copy(j, d).wait_recv()
        gy_copy(j).start()

    def spread_core(j):
        gy_copy(j).wait_recv()
        gc_copy(j).start()

    def finish(j):
        gc_copy(j).wait_recv()
        out_copy(j).start()

    stages = [(0, multiply), (1, add_core), (2, add_y), (4, add_z)]
    if gather:
        stages += [(6, spread_y), (8, spread_core), (9, finish)]

    @pl.loop(0, n + stages[-1][0])
    def _(i):
        for lag, stage in stages:
            @pl.when((i >= lag) & (i < n + lag))
            def _(stage=stage, lag=lag):
                stage(i - lag)

    @pl.loop(0, n)
    def _(j):
        core_copy(j).wait_send()
        y_copy(j).wait_send()
        for d in range(1, zs):
            z_copy(j, d).wait_send()
        if gather:
            for d in range(1, zs):
                gz_copy(j, d).wait_send()
            gy_copy(j).wait_send()
            gc_copy(j).wait_send()
            out_copy(j).wait()


def project(a, weight, residual, zs, gather):
    rows, depth = a.shape
    width = weight.shape[1]
    tok = residual.shape[0]
    n, cw, half = CHUNKS, width // CHUNKS, rows // 2
    dma = pltpu.SemaphoreType.DMA
    vmem = pl.BlockSpec(memory_space=pltpu.VMEM)
    scratch = [
        pltpu.VMEM((n, depth, cw), BF16),
        pltpu.VMEM((n, 2, half, cw), BF16),
        pltpu.VMEM((n, half, cw), BF16),
        pltpu.VMEM((n, 2, half // 2, cw), BF16),
        pltpu.VMEM((n, half // 2, cw), BF16),
        pltpu.VMEM((n, zs, tok, cw), BF16),
        pltpu.VMEM((n, zs, tok, cw), BF16),
        dma((n,)), dma((n,)), dma((n,)), dma((n,)), dma((n,)), dma((n, zs)), dma((n, zs)),
    ]
    outs = [jax.ShapeDtypeStruct((tok, width), BF16)]
    out_specs = [vmem]
    if gather:
        outs.append(jax.ShapeDtypeStruct((n, 2, 2, zs, tok, cw), BF16))
        out_specs.append(pl.BlockSpec(memory_space=pl.ANY))
        scratch += [
            pltpu.VMEM((n, 2, 2, zs, tok, cw), BF16),
            dma((n, zs)), dma((n, zs)), dma((n,)), dma((n,)), dma((n,)), dma((n,)), dma((n,)),
        ]
    res = pl.pallas_call(
        functools.partial(project_kernel, zs, gather),
        out_shape=outs,
        in_specs=[vmem, pl.BlockSpec(memory_space=pl.ANY), vmem],
        out_specs=out_specs,
        scratch_shapes=scratch,
        compiler_params=pltpu.CompilerParams(
            collective_id=0 if gather else 1, has_side_effects=True, vmem_limit_bytes=56 << 20
        ),
        name="attn_out" if gather else "ffn_down",
    )(a, weight, residual)
    return res


def ffn_kernel(which, x_ref, gain_ref, gate_ref, up_ref, hid_ref, inputs):
    n, rows, cw = x_ref.shape
    s = pl.program_id(0)

    @pl.when(s == 0)
    def _():
        block = 64

        @pl.loop(0, rows // block)
        def _(b):
            at = pl.ds(pl.multiple_of(b * block, block), block)
            square = jnp.zeros((block, 1), F32)
            for j in range(n):
                x = x_ref[j, at, :].astype(F32)
                square += jnp.sum(x * x, axis=1, keepdims=True)
            inv = lax.rsqrt(square / (n * cw) + 1e-05)
            for j in range(n):
                x = (x_ref[j, at, :].astype(F32) * inv).astype(BF16).astype(F32)
                for f in range(gain_ref.shape[0]):
                    g = gain_ref[f : f + 1, j * cw : (j + 1) * cw]
                    inputs[f, j, at, :] = (x * g).astype(BF16)

    f = which[s]
    acc = jnp.zeros((rows, 2 * SLICE), F32)
    for j in range(n):
        k = slice(j * cw, (j + 1) * cw)
        both = jnp.concatenate([gate_ref[k, :], up_ref[k, :]], axis=1)
        acc += jnp.dot(inputs[f, j], both, preferred_element_type=F32)
    gate, up = acc[:, :SLICE], acc[:, SLICE:]
    hid_ref[...] = (gate / (1.0 + jnp.exp(-gate)) * up).astype(BF16)


def ffn_hidden(which, x, gain, gate_weight, up_weight):
    n, rows, cw = x.shape
    width, units = gate_weight.shape
    return pl.pallas_call(
        ffn_kernel,
        out_shape=jax.ShapeDtypeStruct((rows, units), BF16),
        grid_spec=pltpu.PrefetchScalarGridSpec(
            num_scalar_prefetch=1,
            grid=(units // SLICE,),
            in_specs=[
                pl.BlockSpec((n, rows, cw), lambda s, w: (0, 0, 0), pipeline_mode=pl.Buffered(1)),
                pl.BlockSpec(gain.shape, lambda s, w: (0, 0), pipeline_mode=pl.Buffered(1)),
                pl.BlockSpec((width, SLICE), lambda s, w: (0, s)),
                pl.BlockSpec((width, SLICE), lambda s, w: (0, s)),
            ],
            out_specs=pl.BlockSpec((rows, SLICE), lambda s, w: (0, s)),
            scratch_shapes=[pltpu.VMEM((gain.shape[0], n, rows, cw), BF16)],
        ),
        compiler_params=pltpu.CompilerParams(vmem_limit_bytes=56 << 20),
        name="ffn_hidden",
    )(which, x, gain, gate_weight, up_weight)


def attention(query_rows, key_cols, value_cols, query_pos, seq_lens, local_heads):
    count = query_rows.shape[0]
    seq_ends = jnp.cumsum(seq_lens)
    key_pos = jnp.arange(count, dtype=jnp.int32)

    def segment_of(positions):
        return jnp.sum((positions[:, None] >= seq_ends[None, :]).astype(jnp.int32), axis=1)

    visible = (segment_of(query_pos)[:, None] == segment_of(key_pos)[None, :]) & (
        key_pos[None, :] <= query_pos[:, None]
    )
    scores = jnp.einsum(
        "thd,sd->hts",
        query_rows.reshape(count, local_heads, HEAD_SIZE),
        key_cols,
        preferred_element_type=F32,
    ) * (1.0 / math.sqrt(HEAD_SIZE))
    masked = jnp.where(visible[None], scores, -1e30)
    highest = jnp.max(masked, axis=-1, keepdims=True)
    expo = jnp.where(visible[None], jnp.exp(masked - highest), 0.0)
    probs = (expo / jnp.sum(expo, axis=-1, keepdims=True)).astype(BF16)
    return (
        jnp.einsum("hts,sd->thd", probs, value_cols, preferred_element_type=F32)
        .astype(BF16)
        .reshape(count, local_heads * HEAD_SIZE)
    )


def local(tokens, queries, key_proj, values, seq_lens, out_weight, ffn_gain, gate_weight, up_weight,
          down_weight, slice_table):
    tok = tokens.shape[0]
    mp = lax.axis_size("mp")
    zs = mp // 4
    count = tok * mp
    me = lax.axis_index("mp")
    heads_kv = key_proj.shape[1] // HEAD_SIZE
    per_group = QUERY_HEADS // heads_kv
    local_heads = QUERY_HEADS // mp

    kv_heads = np.arange(mp) * local_heads // per_group
    repeat = mp // heads_kv
    assert (kv_heads == np.arange(mp) // repeat).all()

    def for_devices(rows):
        return jnp.repeat(rows.reshape(tok, heads_kv, 1, HEAD_SIZE), repeat, axis=2).reshape(
            tok, mp, HEAD_SIZE
        )

    sent = jnp.concatenate(
        [queries.reshape(tok, mp, -1), for_devices(key_proj), for_devices(values)], axis=2
    )
    got = lax.all_to_all(sent.transpose(1, 0, 2), "mp", split_axis=0, concat_axis=0, tiled=True)
    q_width = local_heads * HEAD_SIZE
    key_cols = got[:, :, q_width : q_width + HEAD_SIZE].reshape(count, HEAD_SIZE)
    value_cols = got[:, :, q_width + HEAD_SIZE :].reshape(count, HEAD_SIZE)

    def reorder(rows):
        return rows.reshape(zs, 2, 2, tok, -1).transpose(2, 1, 0, 3, 4)

    query_rows = reorder(got[:, :, :q_width]).reshape(count, q_width)
    query_pos = reorder(jnp.arange(count, dtype=jnp.int32)).reshape(count)
    context = attention(query_rows, key_cols, value_cols, query_pos, seq_lens, local_heads)
    stream, gathered = project(context, out_weight, tokens, zs, True)
    slices = gate_weight.shape[1] // SLICE
    which = lax.dynamic_slice_in_dim(slice_table, me * slices, slices)
    x = gathered.reshape(CHUNKS, count, -1)
    hidden = ffn_hidden(which, x, ffn_gain, gate_weight, up_weight)
    (mixed,) = project(hidden, down_weight, stream, zs, False)
    return (stream, mixed)


def solution(mesh):
    placed = (
        P(("groups", "mp"), None),
        P(("groups", "mp"), None),
        P(("groups", "mp"), None),
        P(("groups", "mp"), None),
        P("groups"),
        P("mp", None),
        P(),
        P(None, "mp"),
        P(None, "mp"),
        P("mp", None),
        P(),
    )
    return jax.shard_map(
        local,
        mesh=mesh,
        in_specs=placed,
        out_specs=(P(("groups", "mp"), None), P(("groups", "mp"), None)),
        check_vma=False,
    )
```

```python
import functools
import math

import jax
import jax.numpy as jnp
import numpy as np
from jax import lax
from jax.experimental import pallas as pl
from jax.experimental.pallas import tpu as pltpu
from jax.sharding import PartitionSpec as P

QUERY_HEADS = 64
HEAD_SIZE = 128
SLICE = 128
CHUNKS = 8
MESH = pl.DeviceIdType.MESH
F32 = jnp.float32
BF16 = jnp.bfloat16


def place(zs):
    me = lax.axis_index("mp")
    core = lax.rem(me, 2)
    y = lax.rem(me // 2, 2)
    z = me // 4

    def dev(z_, y_, core_):
        return {"mp": (z_ * 2 + y_) * 2 + core_}

    return core, y, z, dev


def layer_kernel(zs, slices, *refs):
    (which, a_ref, res_ref, gain_ref, w_hbm, gate_hbm, up_hbm, down_hbm, stream_ref, mixed_ref,
     w, gate, up, part, from_core, pair, from_y, quad, from_z, whole, gained, square, acc, hidden,
     w_sem, gate_sem, up_sem, cs, cr, ys, yr, zsend, zrecv, gzs, gzr, gys, gyr, gcs, gcr) = refs
    core, y, z, dev = place(zs)
    n, half, cw = from_core.shape
    rows = 2 * half
    tok = half // 2 // zs

    def columns(j):
        return pl.ds(pl.multiple_of(j * cw, cw), cw)

    def w_copy(j, first):
        src = w_hbm if first else down_hbm
        dst = w.at[j, pl.ds(0, src.shape[0])]
        return pltpu.make_async_copy(src.at[:, columns(j)], dst, w_sem.at[j])

    def gate_copy(j):
        return pltpu.make_async_copy(gate_hbm.at[columns(j), :], gate.at[j], gate_sem.at[j])

    def up_copy(j):
        return pltpu.make_async_copy(up_hbm.at[columns(j), :], up.at[j], up_sem.at[j])

    def remote(src, dst, s, r, to):
        return pltpu.make_async_remote_copy(
            src_ref=src, dst_ref=dst, send_sem=s, recv_sem=r, device_id=to, device_id_type=MESH
        )

    def core_copy(j):
        return remote(part.at[j, 1 - core], from_core.at[j], cs.at[j], cr.at[j], dev(z, y, 1 - core))

    def y_copy(j):
        return remote(pair.at[j, 1 - y], from_y.at[j], ys.at[j], yr.at[j], dev(z, 1 - y, core))

    def z_copy(j, d):
        to = lax.rem(z + d, zs)
        return remote(
            quad.at[j, to], from_z.at[j, d], zsend.at[j, d], zrecv.at[j, d], dev(to, y, core)
        )

    def gz_copy(j, d):
        to = lax.rem(z + d, zs)
        mine = whole.at[j, core, y, z]
        return remote(mine, mine, gzs.at[j, d], gzr.at[j, d], dev(to, y, core))

    def gy_copy(j):
        mine = whole.at[j, core, y]
        return remote(mine, mine, gys.at[j], gyr.at[j], dev(z, 1 - y, core))

    def gc_copy(j):
        mine = whole.at[j, core]
        return remote(mine, mine, gcs.at[j], gcr.at[j], dev(z, y, 1 - core))

    @pl.loop(0, n)
    def _(j):
        w_copy(j, True).start()

    barrier = pltpu.get_barrier_semaphore()
    partners = [dev(z, y, 1 - core), dev(z, 1 - y, core)]
    partners += [dev(lax.rem(z + d, zs), y, core) for d in range(1, zs)]
    for to in partners:
        pl.semaphore_signal(barrier, inc=1, device_id=to, device_id_type=MESH)
    pl.semaphore_wait(barrier, len(partners))

    @pl.loop(0, n)
    def _(j):
        gate_copy(j).start()
        up_copy(j).start()

    square[...] = jnp.zeros_like(square)
    acc[...] = jnp.zeros_like(acc)

    def multiply(j, first):
        lhs = a_ref if first else hidden
        w_copy(j, first).wait()
        res = jnp.dot(
            lhs[...], w[j, : lhs.shape[1], :], preferred_element_type=F32
        ).astype(BF16)
        part[j, 0] = res[:half]
        part[j, 1] = res[half:]
        core_copy(j).start()
        if first:
            w_copy(j, False).start()

    def add_core(j):
        core_copy(j).wait_recv()
        res = (part[j, core].astype(F32) + from_core[j].astype(F32)).astype(BF16)
        pair[j, 0] = res[: half // 2]
        pair[j, 1] = res[half // 2 :]
        y_copy(j).start()

    def add_y(j):
        y_copy(j).wait_recv()
        res = (pair[j, y].astype(F32) + from_y[j].astype(F32)).astype(BF16)
        quad[j] = res.reshape(zs, tok, cw)
        for d in range(1, zs):
            z_copy(j, d).start()

    def add_z(j, first):
        total = quad[j, z].astype(F32)
        for d in range(1, zs):
            z_copy(j, d).wait_recv()
            total += from_z[j, d].astype(F32)
        before = res_ref if first else stream_ref
        res = (before[:, columns(j)].astype(F32) + total).astype(BF16)
        if first:
            stream_ref[:, columns(j)] = res
            whole[j, core, y, z] = res
            for d in range(1, zs):
                gz_copy(j, d).start()
        else:
            mixed_ref[:, columns(j)] = res

    def spread_y(j):
        for d in range(1, zs):
            gz_copy(j, d).wait_recv()
        gy_copy(j).start()

    def spread_core(j):
        gy_copy(j).wait_recv()
        gc_copy(j).start()

    def consume(j):
        gc_copy(j).wait_recv()
        gate_copy(j).wait()
        up_copy(j).wait()
        for c in range(2):
            for q in range(2):
                x = whole[j, c, q].reshape(zs * tok, cw).astype(F32)
                at = slice((c * 2 + q) * zs * tok, (c * 2 + q + 1) * zs * tok)
                total = square[at, :]
                for k in range(0, cw, 128):
                    total += x[:, k : k + 128] * x[:, k : k + 128]
                square[at, :] = total
                for f in range(gained.shape[0]):
                    gained[f, at, :] = (x * gain_ref[f : f + 1, columns(j)]).astype(BF16)
        for s in range(slices):
            cols = slice(s * SLICE, (s + 1) * SLICE)
            both = jnp.concatenate([gate[j, :, cols], up[j, :, cols]], axis=1)
            acc[s] += jnp.dot(gained[which[s]], both, preferred_element_type=F32)

    def send_waits(j):
        core_copy(j).wait_send()
        y_copy(j).wait_send()
        for d in range(1, zs):
            z_copy(j, d).wait_send()

    def run(stages):
        @pl.loop(0, n + stages[-1][0])
        def _(i):
            for lag, stage in stages:
                @pl.when((i >= lag) & (i < n + lag))
                def _(stage=stage, lag=lag):
                    stage(i - lag)

    run([
        (0, functools.partial(multiply, first=True)), (1, add_core), (2, add_y),
        (4, functools.partial(add_z, first=True)), (6, spread_y), (8, spread_core), (9, consume),
    ])

    inv = lax.rsqrt(jnp.sum(square[...], axis=1, keepdims=True) / (n * cw) + 1e-05)
    for s in range(slices):
        both = acc[s] * inv
        g, u = both[:, :SLICE], both[:, SLICE:]
        hidden[:, s * SLICE : (s + 1) * SLICE] = (g / (1.0 + jnp.exp(-g)) * u).astype(BF16)

    @pl.loop(0, n)
    def _(j):
        send_waits(j)
        for d in range(1, zs):
            gz_copy(j, d).wait_send()
        gy_copy(j).wait_send()
        gc_copy(j).wait_send()

    run([
        (0, functools.partial(multiply, first=False)), (1, add_core), (2, add_y),
        (4, functools.partial(add_z, first=False)),
    ])

    @pl.loop(0, n)
    def _(j):
        send_waits(j)


def layer(which, context, tokens, gain, out_weight, gate_weight, up_weight, down_weight, zs):
    rows, depth = context.shape
    tok, width = tokens.shape
    units = down_weight.shape[0]
    slices = units // SLICE
    n, cw, half = CHUNKS, width // CHUNKS, rows // 2
    dma = pltpu.SemaphoreType.DMA
    vmem = pl.BlockSpec(memory_space=pltpu.VMEM)
    hbm = pl.BlockSpec(memory_space=pl.ANY)
    return pl.pallas_call(
        functools.partial(layer_kernel, zs, slices),
        out_shape=[jax.ShapeDtypeStruct((tok, width), BF16)] * 2,
        in_specs=[pl.BlockSpec(memory_space=pltpu.SMEM)] + [vmem] * 3 + [hbm] * 4,
        out_specs=[vmem] * 2,
        scratch_shapes=[
            pltpu.VMEM((n, max(depth, units), cw), BF16),
            pltpu.VMEM((n, cw, units), BF16),
            pltpu.VMEM((n, cw, units), BF16),
            pltpu.VMEM((n, 2, half, cw), BF16),
            pltpu.VMEM((n, half, cw), BF16),
            pltpu.VMEM((n, 2, half // 2, cw), BF16),
            pltpu.VMEM((n, half // 2, cw), BF16),
            pltpu.VMEM((n, zs, tok, cw), BF16),
            pltpu.VMEM((n, zs, tok, cw), BF16),
            pltpu.VMEM((n, 2, 2, zs, tok, cw), BF16),
            pltpu.VMEM((gain.shape[0], rows, cw), BF16),
            pltpu.VMEM((rows, 128), F32),
            pltpu.VMEM((slices, rows, 2 * SLICE), F32),
            pltpu.VMEM((rows, units), BF16),
            dma((n,)), dma((n,)), dma((n,)),
            dma((n,)), dma((n,)), dma((n,)), dma((n,)), dma((n, zs)), dma((n, zs)),
            dma((n, zs)), dma((n, zs)), dma((n,)), dma((n,)), dma((n,)), dma((n,)),
        ],
        compiler_params=pltpu.CompilerParams(
            collective_id=0, has_side_effects=True, vmem_limit_bytes=60 << 20
        ),
        name="layer",
    )(which, context, tokens, gain, out_weight, gate_weight, up_weight, down_weight)


def attention(query_rows, key_cols, value_cols, query_pos, seq_lens, local_heads):
    count = query_rows.shape[0]
    seq_ends = jnp.cumsum(seq_lens)
    key_pos = jnp.arange(count, dtype=jnp.int32)

    def segment_of(positions):
        return jnp.sum((positions[:, None] >= seq_ends[None, :]).astype(jnp.int32), axis=1)

    visible = (segment_of(query_pos)[:, None] == segment_of(key_pos)[None, :]) & (
        key_pos[None, :] <= query_pos[:, None]
    )
    scores = jnp.einsum(
        "thd,sd->hts",
        query_rows.reshape(count, local_heads, HEAD_SIZE),
        key_cols,
        preferred_element_type=F32,
    ) * (1.0 / math.sqrt(HEAD_SIZE))
    masked = jnp.where(visible[None], scores, -1e30)
    highest = jnp.max(masked, axis=-1, keepdims=True)
    expo = jnp.where(visible[None], jnp.exp(masked - highest), 0.0)
    probs = (expo / jnp.sum(expo, axis=-1, keepdims=True)).astype(BF16)
    return (
        jnp.einsum("hts,sd->thd", probs, value_cols, preferred_element_type=F32)
        .astype(BF16)
        .reshape(count, local_heads * HEAD_SIZE)
    )


def local(tokens, queries, key_proj, values, seq_lens, out_weight, ffn_gain, gate_weight, up_weight,
          down_weight, slice_table):
    tok = tokens.shape[0]
    mp = lax.axis_size("mp")
    zs = mp // 4
    count = tok * mp
    me = lax.axis_index("mp")
    heads_kv = key_proj.shape[1] // HEAD_SIZE
    per_group = QUERY_HEADS // heads_kv
    local_heads = QUERY_HEADS // mp

    kv_heads = np.arange(mp) * local_heads // per_group
    repeat = mp // heads_kv
    assert (kv_heads == np.arange(mp) // repeat).all()

    def for_devices(rows):
        return jnp.repeat(rows.reshape(tok, heads_kv, 1, HEAD_SIZE), repeat, axis=2).reshape(
            tok, mp, HEAD_SIZE
        )

    sent = jnp.concatenate(
        [queries.reshape(tok, mp, -1), for_devices(key_proj), for_devices(values)], axis=2
    )
    got = lax.all_to_all(sent.transpose(1, 0, 2), "mp", split_axis=0, concat_axis=0, tiled=True)
    q_width = local_heads * HEAD_SIZE
    key_cols = got[:, :, q_width : q_width + HEAD_SIZE].reshape(count, HEAD_SIZE)
    value_cols = got[:, :, q_width + HEAD_SIZE :].reshape(count, HEAD_SIZE)

    def reorder(rows):
        return rows.reshape(zs, 2, 2, tok, -1).transpose(2, 1, 0, 3, 4)

    query_rows = reorder(got[:, :, :q_width]).reshape(count, q_width)
    query_pos = reorder(jnp.arange(count, dtype=jnp.int32)).reshape(count)
    context = attention(query_rows, key_cols, value_cols, query_pos, seq_lens, local_heads)
    slices = gate_weight.shape[1] // SLICE
    which = lax.dynamic_slice_in_dim(slice_table, me * slices, slices)
    stream, mixed = layer(
        which, context, tokens, ffn_gain, out_weight, gate_weight, up_weight, down_weight, zs
    )
    return (stream, mixed)


def solution(mesh):
    placed = (
        P(("groups", "mp"), None),
        P(("groups", "mp"), None),
        P(("groups", "mp"), None),
        P(("groups", "mp"), None),
        P("groups"),
        P("mp", None),
        P(),
        P(None, "mp"),
        P(None, "mp"),
        P("mp", None),
        P(),
    )
    return jax.shard_map(
        local,
        mesh=mesh,
        in_specs=placed,
        out_specs=(P(("groups", "mp"), None), P(("groups", "mp"), None)),
        check_vma=False,
    )
```

```python
import functools
import math

import jax
import jax.numpy as jnp
from jax import lax
from jax.experimental import pallas as pl
from jax.experimental.pallas import tpu as pltpu
from jax.sharding import PartitionSpec as P

QUERY_HEADS = 64
HEAD_SIZE = 128
SLICE = 128
CHUNKS = 8
MESH = pl.DeviceIdType.MESH
F32 = jnp.float32
BF16 = jnp.bfloat16


def place(zs):
    me = lax.axis_index("mp")
    core = lax.rem(me, 2)
    y = lax.rem(me // 2, 2)
    z = me // 4

    def dev(z_, y_, core_):
        return {"mp": (z_ * 2 + y_) * 2 + core_}

    return core, y, z, dev


def layer_kernel(zs, slices, *refs):
    (seq_lens, table, q_ref, k_ref, v_ref, res_ref, gain_ref, w_hbm, gate_hbm, up_hbm, down_hbm,
     both_ref, packed, got, a_ref, ps, pr, w, gate, up, part, from_core, pair, from_y, quad, from_z, whole, gained, square, acc, hidden,
     w_sem, gate_sem, up_sem, cs, cr, ys, yr, zsend, zrecv, gzs, gzr, gys, gyr, gcs, gcr) = refs
    core, y, z, dev = place(zs)
    n, half, cw = from_core.shape
    rows = 2 * half
    tok = half // 2 // zs
    mp = 4 * zs
    q_width = packed.shape[2] - 2 * HEAD_SIZE
    me = lax.axis_index("mp")
    stream_ref, mixed_ref = both_ref.at[0], both_ref.at[1]

    def columns(j):
        return pl.ds(pl.multiple_of(j * cw, cw), cw)

    def w_copy(j, first):
        src = w_hbm if first else down_hbm
        dst = w.at[j, pl.ds(0, src.shape[0])]
        return pltpu.make_async_copy(src.at[:, columns(j)], dst, w_sem.at[j])

    def gate_copy(j):
        return pltpu.make_async_copy(gate_hbm.at[columns(j), :], gate.at[j], gate_sem.at[j])

    def up_copy(j):
        return pltpu.make_async_copy(up_hbm.at[columns(j), :], up.at[j], up_sem.at[j])

    def remote(src, dst, s, r, to):
        return pltpu.make_async_remote_copy(
            src_ref=src, dst_ref=dst, send_sem=s, recv_sem=r, device_id=to, device_id_type=MESH
        )

    def core_copy(j):
        return remote(part.at[j, 1 - core], from_core.at[j], cs.at[j], cr.at[j], dev(z, y, 1 - core))

    def y_copy(j):
        return remote(pair.at[j, 1 - y], from_y.at[j], ys.at[j], yr.at[j], dev(z, 1 - y, core))

    def z_copy(j, d):
        to = lax.rem(z + d, zs)
        return remote(
            quad.at[j, to], from_z.at[j, d], zsend.at[j, d], zrecv.at[j, d], dev(to, y, core)
        )

    def gz_copy(j, d):
        to = lax.rem(z + d, zs)
        mine = whole.at[j, core, y, z]
        return remote(mine, mine, gzs.at[j, d], gzr.at[j, d], dev(to, y, core))

    def gy_copy(j):
        mine = whole.at[j, core, y]
        return remote(mine, mine, gys.at[j], gyr.at[j], dev(z, 1 - y, core))

    def gc_copy(j):
        mine = whole.at[j, core]
        return remote(mine, mine, gcs.at[j], gcr.at[j], dev(z, y, 1 - core))

    def head_copy(d):
        to = lax.rem(me + d, mp)
        return remote(packed.at[to], got.at[core, y, z], ps.at[d], pr.at[d], {"mp": to})

    barrier = pltpu.get_barrier_semaphore()

    @pl.loop(1, mp)
    def _(d):
        pl.semaphore_signal(
            barrier, inc=1, device_id={"mp": lax.rem(me + d, mp)}, device_id_type=MESH
        )

    heads_kv = k_ref.shape[1] // HEAD_SIZE
    per_group = QUERY_HEADS // heads_kv
    local_heads = q_width // HEAD_SIZE
    for to in range(mp):
        head = to * local_heads // per_group
        cols = slice(head * HEAD_SIZE, (head + 1) * HEAD_SIZE)
        packed[to, :, :q_width] = q_ref[:, to * q_width : (to + 1) * q_width]
        packed[to, :, q_width : q_width + HEAD_SIZE] = k_ref[:, cols]
        packed[to, :, q_width + HEAD_SIZE :] = v_ref[:, cols]
    got[core, y, z] = packed[me]
    pl.semaphore_wait(barrier, mp - 1)

    @pl.loop(1, mp)
    def _(d):
        head_copy(d).start()

    @pl.loop(0, n)
    def _(j):
        w_copy(j, True).start()

    @pl.loop(0, n)
    def _(j):
        gate_copy(j).start()
        up_copy(j).start()

    def position(at):
        token, z_at = at & (tok - 1), (at // tok) & (zs - 1)
        y_at, core_at = (at // (tok * zs)) & 1, at // (tok * zs * 2)
        return ((z_at * 2 + y_at) * 2 + core_at) * tok + token

    query_pos = position(lax.broadcasted_iota(jnp.int32, (rows, 1), 0))
    key_pos = position(lax.broadcasted_iota(jnp.int32, (1, rows), 1))
    begin = jnp.zeros((rows, 1), jnp.int32)
    end = 0
    for k in range(seq_lens.shape[0]):
        end = end + seq_lens[k]
        begin = jnp.where(query_pos >= end, end, begin)
    visible = (key_pos >= begin) & (key_pos <= query_pos)

    @pl.loop(1, mp)
    def _(d):
        head_copy(d).wait_recv()

    keys = got[:, :, :, :, q_width : q_width + HEAD_SIZE].reshape(rows, HEAD_SIZE)
    vals = got[:, :, :, :, q_width + HEAD_SIZE :].reshape(rows, HEAD_SIZE)
    for h in range(local_heads):
        cols = slice(h * HEAD_SIZE, (h + 1) * HEAD_SIZE)
        heads = got[:, :, :, :, cols].reshape(rows, HEAD_SIZE)
        scores = lax.dot_general(
            heads, keys, (((1,), (1,)), ((), ())), preferred_element_type=F32
        ) * (1.0 / math.sqrt(HEAD_SIZE))
        masked = jnp.where(visible, scores, -1e30)
        highest = jnp.max(masked, axis=1, keepdims=True)
        expo = jnp.where(visible, jnp.exp(masked - highest), 0.0)
        probs = (expo / jnp.sum(expo, axis=1, keepdims=True)).astype(BF16)
        a_ref[:, cols] = jnp.dot(probs, vals, preferred_element_type=F32).astype(BF16)

    @pl.loop(1, mp)
    def _(d):
        head_copy(d).wait_send()

    square[...] = jnp.zeros_like(square)
    acc[...] = jnp.zeros_like(acc)

    def multiply(j, first):
        lhs = a_ref if first else hidden
        w_copy(j, first).wait()
        res = jnp.dot(
            lhs[...], w[j, : lhs.shape[1], :], preferred_element_type=F32
        ).astype(BF16)
        part[j, 0] = res[:half]
        part[j, 1] = res[half:]
        core_copy(j).start()
        if first:
            w_copy(j, False).start()

    def add_core(j):
        core_copy(j).wait_recv()
        res = (part[j, core].astype(F32) + from_core[j].astype(F32)).astype(BF16)
        pair[j, 0] = res[: half // 2]
        pair[j, 1] = res[half // 2 :]
        y_copy(j).start()

    def add_y(j):
        y_copy(j).wait_recv()
        res = (pair[j, y].astype(F32) + from_y[j].astype(F32)).astype(BF16)
        quad[j] = res.reshape(zs, tok, cw)
        for d in range(1, zs):
            z_copy(j, d).start()

    def add_z(j, first):
        total = quad[j, z].astype(F32)
        for d in range(1, zs):
            z_copy(j, d).wait_recv()
            total += from_z[j, d].astype(F32)
        before = res_ref if first else stream_ref
        res = (before[:, columns(j)].astype(F32) + total).astype(BF16)
        if first:
            stream_ref[:, columns(j)] = res
            whole[j, core, y, z] = res
            for d in range(1, zs):
                gz_copy(j, d).start()
        else:
            mixed_ref[:, columns(j)] = res

    def spread_y(j):
        for d in range(1, zs):
            gz_copy(j, d).wait_recv()
        gy_copy(j).start()

    def spread_core(j):
        gy_copy(j).wait_recv()
        gc_copy(j).start()

    def consume(j):
        gc_copy(j).wait_recv()
        gate_copy(j).wait()
        up_copy(j).wait()
        for c in range(2):
            for q in range(2):
                x = whole[j, c, q].reshape(zs * tok, cw).astype(F32)
                at = slice((c * 2 + q) * zs * tok, (c * 2 + q + 1) * zs * tok)
                total = square[at, :]
                for k in range(0, cw, 128):
                    total += x[:, k : k + 128] * x[:, k : k + 128]
                square[at, :] = total
                for f in range(gained.shape[0]):
                    gained[f, at, :] = (x * gain_ref[f : f + 1, columns(j)]).astype(BF16)
        for s in range(slices):
            cols = slice(s * SLICE, (s + 1) * SLICE)
            both = jnp.concatenate([gate[j, :, cols], up[j, :, cols]], axis=1)
            acc[s] += jnp.dot(gained[table[me * slices + s]], both, preferred_element_type=F32)

    def send_waits(j):
        core_copy(j).wait_send()
        y_copy(j).wait_send()
        for d in range(1, zs):
            z_copy(j, d).wait_send()

    def run(stages):
        @pl.loop(0, n + stages[-1][0])
        def _(i):
            for lag, stage in stages:
                @pl.when((i >= lag) & (i < n + lag))
                def _(stage=stage, lag=lag):
                    stage(i - lag)

    run([
        (0, functools.partial(multiply, first=True)), (1, add_core), (2, add_y),
        (4, functools.partial(add_z, first=True)), (6, spread_y), (8, spread_core), (9, consume),
    ])

    inv = lax.rsqrt(jnp.sum(square[...], axis=1, keepdims=True) / (n * cw) + 1e-05)
    for s in range(slices):
        both = acc[s] * inv
        g, u = both[:, :SLICE], both[:, SLICE:]
        hidden[:, s * SLICE : (s + 1) * SLICE] = (g / (1.0 + jnp.exp(-g)) * u).astype(BF16)

    @pl.loop(0, n)
    def _(j):
        send_waits(j)
        for d in range(1, zs):
            gz_copy(j, d).wait_send()
        gy_copy(j).wait_send()
        gc_copy(j).wait_send()

    run([
        (0, functools.partial(multiply, first=False)), (1, add_core), (2, add_y),
        (4, functools.partial(add_z, first=False)),
    ])

    @pl.loop(0, n)
    def _(j):
        send_waits(j)


def layer(seq_lens, table, queries, keys, vals, tokens, gain, out_weight, gate_weight, up_weight,
          down_weight, zs):
    tok, width = tokens.shape
    depth = out_weight.shape[0]
    mp = 4 * zs
    rows = tok * mp
    assert tok & (tok - 1) == 0 and zs & (zs - 1) == 0
    units = down_weight.shape[0]
    slices = units // SLICE
    n, cw, half = CHUNKS, width // CHUNKS, rows // 2
    dma = pltpu.SemaphoreType.DMA
    vmem = pl.BlockSpec(memory_space=pltpu.VMEM)
    hbm = pl.BlockSpec(memory_space=pl.ANY)
    return pl.pallas_call(
        functools.partial(layer_kernel, zs, slices),
        out_shape=jax.ShapeDtypeStruct((2, tok, width), BF16),
        in_specs=[pl.BlockSpec(memory_space=pltpu.SMEM)] * 2 + [vmem] * 5 + [hbm] * 4,
        out_specs=vmem,
        scratch_shapes=[
            pltpu.VMEM((mp, tok, depth + 2 * HEAD_SIZE), BF16),
            pltpu.VMEM((2, 2, zs, tok, depth + 2 * HEAD_SIZE), BF16),
            pltpu.VMEM((rows, depth), BF16),
            dma((mp,)), dma((mp,)),
            pltpu.VMEM((n, max(depth, units), cw), BF16),
            pltpu.VMEM((n, cw, units), BF16),
            pltpu.VMEM((n, cw, units), BF16),
            pltpu.VMEM((n, 2, half, cw), BF16),
            pltpu.VMEM((n, half, cw), BF16),
            pltpu.VMEM((n, 2, half // 2, cw), BF16),
            pltpu.VMEM((n, half // 2, cw), BF16),
            pltpu.VMEM((n, zs, tok, cw), BF16),
            pltpu.VMEM((n, zs, tok, cw), BF16),
            pltpu.VMEM((n, 2, 2, zs, tok, cw), BF16),
            pltpu.VMEM((gain.shape[0], rows, cw), BF16),
            pltpu.VMEM((rows, 128), F32),
            pltpu.VMEM((slices, rows, 2 * SLICE), F32),
            pltpu.VMEM((rows, units), BF16),
            dma((n,)), dma((n,)), dma((n,)),
            dma((n,)), dma((n,)), dma((n,)), dma((n,)), dma((n, zs)), dma((n, zs)),
            dma((n, zs)), dma((n, zs)), dma((n,)), dma((n,)), dma((n,)), dma((n,)),
        ],
        compiler_params=pltpu.CompilerParams(
            collective_id=0, has_side_effects=True, vmem_limit_bytes=60 << 20
        ),
        name="layer",
    )(seq_lens, table, queries, keys, vals, tokens, gain, out_weight, gate_weight, up_weight, down_weight)


def local(tokens, queries, key_proj, values, seq_lens, out_weight, ffn_gain, gate_weight, up_weight,
          down_weight, slice_table):
    both = layer(
        seq_lens, slice_table, queries, key_proj, values, tokens, ffn_gain, out_weight, gate_weight,
        up_weight, down_weight, lax.axis_size("mp") // 4
    )
    stream, mixed = both[0], both[1]
    return (stream, mixed)


def solution(mesh):
    placed = (
        P(("groups", "mp"), None),
        P(("groups", "mp"), None),
        P(("groups", "mp"), None),
        P(("groups", "mp"), None),
        P("groups"),
        P("mp", None),
        P(),
        P(None, "mp"),
        P(None, "mp"),
        P("mp", None),
        P(),
    )
    return jax.shard_map(
        local,
        mesh=mesh,
        in_specs=placed,
        out_specs=(P(("groups", "mp"), None), P(("groups", "mp"), None)),
        check_vma=False,
    )
```

```python
import functools
import math

import jax
import jax.numpy as jnp
from jax import lax
from jax.experimental import pallas as pl
from jax.experimental.pallas import tpu as pltpu
from jax.sharding import PartitionSpec as P

QUERY_HEADS = 64
HEAD_SIZE = 128
SLICE = 128
CHUNKS = 8
MESH = pl.DeviceIdType.MESH
F32 = jnp.float32
BF16 = jnp.bfloat16


def place(zs):
    me = lax.axis_index("mp")
    core = lax.rem(me, 2)
    y = lax.rem(me // 2, 2)
    z = me // 4

    def dev(z_, y_, core_):
        return {"mp": (z_ * 2 + y_) * 2 + core_}

    return core, y, z, dev


def layer_kernel(zs, slices, *refs):
    (seq_lens, table, q_ref, k_ref, v_ref, res_ref, gain_ref, w_hbm, gate_hbm, up_hbm, down_hbm,
     both_ref, packed, got, a_ref, ps, pr, w, gate, up, part, from_core, pair, from_y, quad, from_z, whole, gained, square, acc, hidden,
     w_sem, gate_sem, up_sem, cs, cr, ys, yr, zsend, zrecv, gzs, gzr, gys, gyr, gcs, gcr) = refs
    core, y, z, dev = place(zs)
    n, half, cw = from_core.shape
    rows = 2 * half
    tok = half // 2 // zs
    mp = 4 * zs
    q_width = packed.shape[2] - 2 * HEAD_SIZE
    me = lax.axis_index("mp")
    stream_ref, mixed_ref = both_ref.at[0], both_ref.at[1]

    def columns(j):
        return pl.ds(pl.multiple_of(j * cw, cw), cw)

    def w_copy(j, first):
        src = w_hbm if first else down_hbm
        dst = w.at[j, pl.ds(0, src.shape[0])]
        return pltpu.make_async_copy(src.at[:, columns(j)], dst, w_sem.at[j])

    def gate_copy(j):
        return pltpu.make_async_copy(gate_hbm.at[columns(j), :], gate.at[j], gate_sem.at[j])

    def up_copy(j):
        return pltpu.make_async_copy(up_hbm.at[columns(j), :], up.at[j], up_sem.at[j])

    def remote(src, dst, s, r, to):
        return pltpu.make_async_remote_copy(
            src_ref=src, dst_ref=dst, send_sem=s, recv_sem=r, device_id=to, device_id_type=MESH
        )

    def core_copy(j):
        return remote(part.at[j, 1 - core], from_core.at[j], cs.at[j], cr.at[j], dev(z, y, 1 - core))

    def y_copy(j):
        return remote(pair.at[j, 1 - y], from_y.at[j], ys.at[j], yr.at[j], dev(z, 1 - y, core))

    def z_copy(j, d):
        to = lax.rem(z + d, zs)
        return remote(
            quad.at[j, to], from_z.at[j, d], zsend.at[j, d], zrecv.at[j, d], dev(to, y, core)
        )

    def gz_copy(j, d):
        to = lax.rem(z + d, zs)
        mine = whole.at[j, core, y, z]
        return remote(mine, mine, gzs.at[j, d], gzr.at[j, d], dev(to, y, core))

    def gy_copy(j):
        mine = whole.at[j, core, y]
        return remote(mine, mine, gys.at[j], gyr.at[j], dev(z, 1 - y, core))

    def gc_copy(j):
        mine = whole.at[j, core]
        return remote(mine, mine, gcs.at[j], gcr.at[j], dev(z, y, 1 - core))

    def head_copy(d):
        to = lax.rem(me + d, mp)
        return remote(packed.at[to], got.at[core, y, z], ps.at[d], pr.at[d], {"mp": to})

    @pl.loop(0, n)
    def _(j):
        w_copy(j, True).start()

    barrier = pltpu.get_barrier_semaphore()

    @pl.loop(1, mp)
    def _(d):
        pl.semaphore_signal(
            barrier, inc=1, device_id={"mp": lax.rem(me + d, mp)}, device_id_type=MESH
        )

    heads_kv = k_ref.shape[1] // HEAD_SIZE
    per_group = QUERY_HEADS // heads_kv
    local_heads = q_width // HEAD_SIZE
    for to in range(mp):
        head = to * local_heads // per_group
        cols = slice(head * HEAD_SIZE, (head + 1) * HEAD_SIZE)
        packed[to, :, :q_width] = q_ref[:, to * q_width : (to + 1) * q_width]
        packed[to, :, q_width : q_width + HEAD_SIZE] = k_ref[:, cols]
        packed[to, :, q_width + HEAD_SIZE :] = v_ref[:, cols]
    got[core, y, z] = packed[me]
    pl.semaphore_wait(barrier, mp - 1)

    @pl.loop(0, mp - 1)
    def _(i):
        head_copy(lax.rem(i + mp // 2 - 1, mp - 1) + 1).start()

    @pl.loop(0, n)
    def _(j):
        gate_copy(j).start()
        up_copy(j).start()

    def position(at):
        token, z_at = at & (tok - 1), (at // tok) & (zs - 1)
        y_at, core_at = (at // (tok * zs)) & 1, at // (tok * zs * 2)
        return ((z_at * 2 + y_at) * 2 + core_at) * tok + token

    query_pos = position(lax.broadcasted_iota(jnp.int32, (rows, 1), 0))
    key_pos = position(lax.broadcasted_iota(jnp.int32, (1, rows), 1))
    begin = jnp.zeros((rows, 1), jnp.int32)
    end = 0
    for k in range(seq_lens.shape[0]):
        end = end + seq_lens[k]
        begin = jnp.where(query_pos >= end, end, begin)
    visible = (key_pos >= begin) & (key_pos <= query_pos)

    @pl.loop(1, mp)
    def _(d):
        head_copy(d).wait_recv()

    keys = got[:, :, :, :, q_width : q_width + HEAD_SIZE].reshape(rows, HEAD_SIZE)
    vals = got[:, :, :, :, q_width + HEAD_SIZE :].reshape(rows, HEAD_SIZE)
    for h in range(local_heads):
        cols = slice(h * HEAD_SIZE, (h + 1) * HEAD_SIZE)
        heads = got[:, :, :, :, cols].reshape(rows, HEAD_SIZE)
        scores = lax.dot_general(
            heads, keys, (((1,), (1,)), ((), ())), preferred_element_type=F32
        ) * (1.0 / math.sqrt(HEAD_SIZE))
        masked = jnp.where(visible, scores, -1e30)
        highest = jnp.max(masked, axis=1, keepdims=True)
        expo = jnp.where(visible, jnp.exp(masked - highest), 0.0)
        probs = (expo / jnp.sum(expo, axis=1, keepdims=True)).astype(BF16)
        a_ref[:, cols] = jnp.dot(probs, vals, preferred_element_type=F32).astype(BF16)

    @pl.loop(1, mp)
    def _(d):
        head_copy(d).wait_send()

    square[...] = jnp.zeros_like(square)
    acc[...] = jnp.zeros_like(acc)

    def multiply(j, first):
        lhs = a_ref if first else hidden
        w_copy(j, first).wait()
        res = jnp.dot(
            lhs[...], w[j, : lhs.shape[1], :], preferred_element_type=F32
        ).astype(BF16)
        part[j, 0] = res[:half]
        part[j, 1] = res[half:]
        core_copy(j).start()
        if first:
            w_copy(j, False).start()

    def add_core(j):
        core_copy(j).wait_recv()
        res = (part[j, core].astype(F32) + from_core[j].astype(F32)).astype(BF16)
        pair[j, 0] = res[: half // 2]
        pair[j, 1] = res[half // 2 :]
        y_copy(j).start()

    def add_y(j):
        y_copy(j).wait_recv()
        res = (pair[j, y].astype(F32) + from_y[j].astype(F32)).astype(BF16)
        quad[j] = res.reshape(zs, tok, cw)
        for d in range(1, zs):
            z_copy(j, d).start()

    def add_z(j, first):
        total = quad[j, z].astype(F32)
        for d in range(1, zs):
            z_copy(j, d).wait_recv()
            total += from_z[j, d].astype(F32)
        before = res_ref if first else stream_ref
        res = (before[:, columns(j)].astype(F32) + total).astype(BF16)
        if first:
            stream_ref[:, columns(j)] = res
            whole[j, core, y, z] = res
            for d in range(1, zs):
                gz_copy(j, d).start()
        else:
            mixed_ref[:, columns(j)] = res

    def spread_y(j):
        for d in range(1, zs):
            gz_copy(j, d).wait_recv()
        gy_copy(j).start()

    def spread_core(j):
        gy_copy(j).wait_recv()
        gc_copy(j).start()

    def consume(j):
        gc_copy(j).wait_recv()
        gate_copy(j).wait()
        up_copy(j).wait()
        for c in range(2):
            for q in range(2):
                x = whole[j, c, q].reshape(zs * tok, cw).astype(F32)
                at = slice((c * 2 + q) * zs * tok, (c * 2 + q + 1) * zs * tok)
                total = square[at, :]
                for k in range(0, cw, 128):
                    total += x[:, k : k + 128] * x[:, k : k + 128]
                square[at, :] = total
                for f in range(gained.shape[0]):
                    gained[f, at, :] = (x * gain_ref[f : f + 1, columns(j)]).astype(BF16)
        for s in range(slices):
            cols = slice(s * SLICE, (s + 1) * SLICE)
            both = jnp.concatenate([gate[j, :, cols], up[j, :, cols]], axis=1)
            acc[s] += jnp.dot(gained[table[me * slices + s]], both, preferred_element_type=F32)

    def send_waits(j):
        core_copy(j).wait_send()
        y_copy(j).wait_send()
        for d in range(1, zs):
            z_copy(j, d).wait_send()

    def run(stages):
        @pl.loop(0, n + stages[-1][0])
        def _(i):
            for lag, stage in stages:
                @pl.when((i >= lag) & (i < n + lag))
                def _(stage=stage, lag=lag):
                    stage(i - lag)

    run([
        (0, functools.partial(multiply, first=True)), (1, add_core), (2, add_y),
        (4, functools.partial(add_z, first=True)), (6, spread_y), (8, spread_core), (9, consume),
    ])

    inv = lax.rsqrt(jnp.sum(square[...], axis=1, keepdims=True) / (n * cw) + 1e-05)
    for s in range(slices):
        both = acc[s] * inv
        g, u = both[:, :SLICE], both[:, SLICE:]
        hidden[:, s * SLICE : (s + 1) * SLICE] = (g / (1.0 + jnp.exp(-g)) * u).astype(BF16)

    @pl.loop(0, n)
    def _(j):
        send_waits(j)
        for d in range(1, zs):
            gz_copy(j, d).wait_send()
        gy_copy(j).wait_send()
        gc_copy(j).wait_send()

    run([
        (0, functools.partial(multiply, first=False)), (1, add_core), (2, add_y),
        (4, functools.partial(add_z, first=False)),
    ])

    @pl.loop(0, n)
    def _(j):
        send_waits(j)


def layer(seq_lens, table, queries, keys, vals, tokens, gain, out_weight, gate_weight, up_weight,
          down_weight, zs):
    tok, width = tokens.shape
    depth = out_weight.shape[0]
    mp = 4 * zs
    rows = tok * mp
    assert tok & (tok - 1) == 0 and zs & (zs - 1) == 0
    units = down_weight.shape[0]
    slices = units // SLICE
    n, cw, half = CHUNKS, width // CHUNKS, rows // 2
    dma = pltpu.SemaphoreType.DMA
    vmem = pl.BlockSpec(memory_space=pltpu.VMEM)
    hbm = pl.BlockSpec(memory_space=pl.ANY)
    return pl.pallas_call(
        functools.partial(layer_kernel, zs, slices),
        out_shape=jax.ShapeDtypeStruct((2, tok, width), BF16),
        in_specs=[pl.BlockSpec(memory_space=pltpu.SMEM)] * 2 + [vmem] * 5 + [hbm] * 4,
        out_specs=vmem,
        scratch_shapes=[
            pltpu.VMEM((mp, tok, depth + 2 * HEAD_SIZE), BF16),
            pltpu.VMEM((2, 2, zs, tok, depth + 2 * HEAD_SIZE), BF16),
            pltpu.VMEM((rows, depth), BF16),
            dma((mp,)), dma((mp,)),
            pltpu.VMEM((n, max(depth, units), cw), BF16),
            pltpu.VMEM((n, cw, units), BF16),
            pltpu.VMEM((n, cw, units), BF16),
            pltpu.VMEM((n, 2, half, cw), BF16),
            pltpu.VMEM((n, half, cw), BF16),
            pltpu.VMEM((n, 2, half // 2, cw), BF16),
            pltpu.VMEM((n, half // 2, cw), BF16),
            pltpu.VMEM((n, zs, tok, cw), BF16),
            pltpu.VMEM((n, zs, tok, cw), BF16),
            pltpu.VMEM((n, 2, 2, zs, tok, cw), BF16),
            pltpu.VMEM((gain.shape[0], rows, cw), BF16),
            pltpu.VMEM((rows, 128), F32),
            pltpu.VMEM((slices, rows, 2 * SLICE), F32),
            pltpu.VMEM((rows, units), BF16),
            dma((n,)), dma((n,)), dma((n,)),
            dma((n,)), dma((n,)), dma((n,)), dma((n,)), dma((n, zs)), dma((n, zs)),
            dma((n, zs)), dma((n, zs)), dma((n,)), dma((n,)), dma((n,)), dma((n,)),
        ],
        compiler_params=pltpu.CompilerParams(
            collective_id=0, has_side_effects=True, vmem_limit_bytes=60 << 20
        ),
        name="layer",
    )(seq_lens, table, queries, keys, vals, tokens, gain, out_weight, gate_weight, up_weight, down_weight)


def local(tokens, queries, key_proj, values, seq_lens, out_weight, ffn_gain, gate_weight, up_weight,
          down_weight, slice_table):
    both = layer(
        seq_lens, slice_table, queries, key_proj, values, tokens, ffn_gain, out_weight, gate_weight,
        up_weight, down_weight, lax.axis_size("mp") // 4
    )
    stream, mixed = both[0], both[1]
    return (stream, mixed)


def solution(mesh):
    placed = (
        P(("groups", "mp"), None),
        P(("groups", "mp"), None),
        P(("groups", "mp"), None),
        P(("groups", "mp"), None),
        P("groups"),
        P("mp", None),
        P(),
        P(None, "mp"),
        P(None, "mp"),
        P("mp", None),
        P(),
    )
    return jax.shard_map(
        local,
        mesh=mesh,
        in_specs=placed,
        out_specs=(P(("groups", "mp"), None), P(("groups", "mp"), None)),
        check_vma=False,
    )
```
